512 devices in a mesh: ctx: 64 (over x, z), kvh: 8 (over y, core).
Axes of the slice: x: 4, y: 4, z: 16, core: 2. Of those that a mesh axis runs over, the one named last changes fastest.
Arguments:
- queries: bfloat16 [16384, 8192], P(('ctx', 'kvh')), may hold values from -36 to 36
- keys: bfloat16 [16384, 1024], P(('ctx', 'kvh')), may hold values from -4 to 4
- values: bfloat16 [16384, 1024], P(('ctx', 'kvh')), may hold values from -6 to 6
- documents: int32 [16384], replicated, may hold values from 0 to 84, never falling along the last dimension, each value on 1 to 768 neighbouring positions
- grad_out: bfloat16 [16384, 8192], P(('ctx', 'kvh')), may hold values from -6 to 6
Outputs:
- attended: bfloat16 [16384, 8192], P(('ctx', 'kvh'))
- grad_queries: bfloat16 [16384, 8192], P(('ctx', 'kvh'))
- grad_keys: bfloat16 [16384, 1024], P(('ctx', 'kvh'))
- grad_values: bfloat16 [16384, 1024], P(('ctx', 'kvh'))
The draws below stay inside these ranges and needn't reach their ends.
Inputs may be any that keep to these rules, and one draw needn't show every extreme that they name: `documents`: document numbers never fall along the window; every document has 1 to 768 positions, and one has exactly 768.
All inputs are finite; a program needn't handle non-finite values.
Results may differ from the reference program's by a relative error of at most 0.03.
Values may be sent and summed in bfloat16 or wider, within the bound.
A program may use at most 64 MiB of HBM per device.

```python
import math
import jax
import jax.numpy as jnp
import numpy as np
from jax import lax

KVH = 8
GROUP = 8
HD = 128
TOK_DEV = 256
REACH = 3
QH = 64
TOKENS = 16384
MOST = 768
DOCS = 85


def key_field(key):
    field = jnp.clip(jax.random.normal(jax.random.fold_in(key, 23), (TOKENS, KVH * HD), jnp.float32), -4.0, 4.0)
    return field


def draw_keys(key, part):
    return key_field(key).astype(jnp.bfloat16)


def draw_queries(key, part):
    field = jnp.clip(jax.random.normal(jax.random.fold_in(key, 37), (TOKENS, QH * HD), jnp.float32), -4.0, 4.0)
    return field.astype(jnp.bfloat16)


def levels(own_key, dims, split, low, largest):
    gain, own = 1.0, jax.random.fold_in(own_key, 6)
    for position, parts in split:
        steps = jnp.exp(jax.random.uniform(jax.random.fold_in(own, position), (parts,), jnp.float32, low / len(split), largest / len(split)))
        gain = gain * jnp.repeat(steps, dims[position] // parts).reshape([-1 if axis == position else 1 for axis in range(len(dims))])
    return gain


def length_profile(amount, total, bound, lean):
    portions = [(1 << 20) // math.isqrt(rank ** lean) + 1 for rank in range(2, amount + 1)]
    rest, counts = total - bound - (amount - 1), [1] * (amount - 1)
    while rest > 0:
        movable = [i for i in range(amount - 1) if counts[i] < bound]
        mass, left = sum([portions[i] for i in movable]), rest
        for i in movable:
            more = min(bound - counts[i], max(1, left * portions[i] // mass), rest)
            counts[i] = counts[i] + more
            rest = rest - more
    return np.array([bound] + counts)


def ragged(rng, number_of, total, bound, slope):
    if number_of == 2:
        one = jax.random.randint(rng, (), max(1, total - bound), min(bound, total - 1) + 1)
        return jnp.stack([one, total - one])
    sizes = jnp.asarray(length_profile(number_of, total, bound, slope), jnp.int32)
    pairs = (number_of - 1) // 2
    source_of, receiver = sizes[1:1 + 2 * pairs:2], sizes[2:2 + 2 * pairs:2]
    room = jnp.minimum(source_of - 1, bound - receiver)
    moved = jax.random.randint(jax.random.fold_in(rng, 1), (pairs,), 0, 1 << 20) % (room + 1)
    sizes = sizes.at[1:1 + 2 * pairs:2].set(source_of - moved).at[2:2 + 2 * pairs:2].set(receiver + moved)
    return sizes[jax.random.permutation(jax.random.fold_in(rng, 2), number_of)]


def normal_values(stream_key, shape, deviation, bound, cuts=(), held_as=jnp.bfloat16):
    factor_of = levels(stream_key, shape, cuts, -0.22, 0.18) if cuts else 1.0
    array = jax.random.normal(stream_key, shape, jnp.float32) * deviation * factor_of
    return jnp.minimum(jnp.maximum(array, -bound), bound).astype(held_as)


def setup_inputs(seed: int = 0) -> dict:
    key_of = jax.random.split(jax.random.key(seed), 6)
    queries = draw_queries(jax.random.fold_in(key_of[5], 71), 0)
    keys = draw_keys(jax.random.fold_in(key_of[5], 71), 0)
    values = normal_values(key_of[2], (TOKENS, KVH * HD), 1.0, 6.0, ((0, 512),))
    documents = jnp.searchsorted(jnp.cumsum(ragged(key_of[3], DOCS, TOKENS, MOST, 2)), jnp.arange(TOKENS), side="right").astype(jnp.int32)
    grad_out = normal_values(key_of[4], (TOKENS, QH * HD), 1.0, 6.0, ((0, 512),))
    return dict(queries=queries, keys=keys, values=values, documents=documents, grad_out=grad_out)


def block_terms(query_block, grad_block, key_window, value_window, visible):
    scale = 1.0 / math.sqrt(HD)
    highest = lax.Precision.HIGHEST
    query_float = query_block.astype(jnp.float32)
    grad_float = grad_block.astype(jnp.float32)
    key_float = key_window.astype(jnp.float32)
    value_float = value_window.astype(jnp.float32)
    seen = visible[None, None, :, :]
    scores = scale * jnp.einsum('qhgd,khd->hgqk', query_float, key_float, precision=highest)
    masked = jnp.where(seen, scores, -jnp.inf)
    peak = lax.optimization_barrier(jnp.max(masked, axis=-1, keepdims=True))
    summed = lax.optimization_barrier(jnp.sum(jnp.where(seen, jnp.exp(masked - peak), 0.0), axis=-1, keepdims=True))
    log_total = peak + jnp.log(summed)
    probs = jnp.where(seen, jnp.exp(scores - log_total), 0.0)
    weights_low = probs.astype(jnp.bfloat16)
    weights_float = weights_low.astype(jnp.float32)
    attended = jnp.einsum('hgqk,khd->qhgd', weights_float, value_float, precision=highest).astype(jnp.bfloat16)
    delta = lax.optimization_barrier(jnp.sum(grad_float * attended.astype(jnp.float32), axis=-1))
    delta = jnp.transpose(delta, (1, 2, 0))[..., None]
    grad_weights = jnp.einsum('qhgd,khd->hgqk', grad_float, value_float, precision=highest)
    grad_scores = (probs * (grad_weights - delta)).astype(jnp.bfloat16).astype(jnp.float32)
    grad_queries = (scale * jnp.einsum('hgqk,khd->qhgd', grad_scores, key_float, precision=highest)).astype(jnp.bfloat16)
    grad_keys = scale * jnp.einsum('hgqk,qhgd->khd', grad_scores, query_float, precision=highest)
    grad_values = jnp.einsum('hgqk,qhgd->khd', weights_float, grad_float, precision=highest)
    return (attended, grad_queries, grad_keys, grad_values)

def reference(queries, keys, values, documents, grad_out):
    margin = REACH * TOK_DEV
    width = margin + TOK_DEV
    shards = TOKENS // TOK_DEV
    query_four = queries.reshape(TOKENS, KVH, GROUP, HD)
    grad_four = grad_out.reshape(TOKENS, KVH, GROUP, HD)
    key_three = jnp.concatenate([jnp.zeros((margin, KVH, HD), keys.dtype), keys.reshape(TOKENS, KVH, HD)], 0)
    value_three = jnp.concatenate([jnp.zeros((margin, KVH, HD), values.dtype), values.reshape(TOKENS, KVH, HD)], 0)
    padded_docs = jnp.concatenate([jnp.full((margin,), -1, jnp.int32), documents.astype(jnp.int32)])

    def one_block(carry, index):
        key_grads, value_grads = carry
        start = (index * TOK_DEV).astype(jnp.int32)
        query_block = lax.dynamic_slice_in_dim(query_four, start, TOK_DEV, 0)
        grad_block = lax.dynamic_slice_in_dim(grad_four, start, TOK_DEV, 0)
        key_window = lax.dynamic_slice_in_dim(key_three, start, width, 0)
        value_window = lax.dynamic_slice_in_dim(value_three, start, width, 0)
        query_docs = lax.dynamic_slice_in_dim(padded_docs, start + margin, TOK_DEV, 0)
        key_docs = lax.dynamic_slice_in_dim(padded_docs, start, width, 0)
        query_pos = margin + jnp.arange(TOK_DEV, dtype=jnp.int32)
        key_pos = jnp.arange(width, dtype=jnp.int32)
        visible = (key_docs[None, :] == query_docs[:, None]) & (key_pos[None, :] <= query_pos[:, None])
        attended, grad_queries, grad_keys, grad_values = block_terms(query_block, grad_block, key_window, value_window, visible)
        key_grads = lax.dynamic_update_slice_in_dim(key_grads, lax.dynamic_slice_in_dim(key_grads, start, width, 0) + grad_keys, start, 0)
        value_grads = lax.dynamic_update_slice_in_dim(value_grads, lax.dynamic_slice_in_dim(value_grads, start, width, 0) + grad_values, start, 0)
        return ((key_grads, value_grads), (attended, grad_queries))
    initial = (jnp.zeros((TOKENS + margin, KVH, HD), jnp.float32), jnp.zeros((TOKENS + margin, KVH, HD), jnp.float32))
    carry, stacked = lax.scan(one_block, initial, jnp.arange(shards, dtype=jnp.int32))
    attended = stacked[0].reshape(TOKENS, QH * HD)
    grad_queries = stacked[1].reshape(TOKENS, QH * HD)
    grad_keys = carry[0][margin:].reshape(TOKENS, KVH * HD).astype(jnp.bfloat16)
    grad_values = carry[1][margin:].reshape(TOKENS, KVH * HD).astype(jnp.bfloat16)
    return (attended, grad_queries, grad_keys, grad_values)
```

```python
import math

import jax
import jax.numpy as jnp
from jax import lax
from jax.experimental import pallas as pl
from jax.experimental.pallas import tpu as pltpu
from jax.sharding import PartitionSpec as P

HD = 128
REACH = 3
PEERS = 8
ROWS = 32
SHARD = 256
WIN = 1024
SPAN = 896
GW = 1024
SCALE = 1.0 / math.sqrt(HD)
LOG2E = 1.4426950408889634
MESH = pl.DeviceIdType.MESH
F32 = jnp.float32
BF16 = jnp.bfloat16
NT = (((1,), (1,)), ((), ()))
NN = (((1,), (0,)), ((), ()))


def dot(a, b, dims=NN):
    return lax.dot_general(a, b, dims, preferred_element_type=F32)


def kernel(
    q_ref, k_ref, v_ref, doc_ref, go_ref,
    att_ref, gq_ref, gk_ref, gv_ref,
    qb, gb, kw, vw, kt, vt, qall, got, kd, bias, scr, eall, dsall, ob, gqb,
    part, sendk, recvk, fin,
    q_s, q_r, kv_s, kv_r, z_s, z_r, o_s, o_r, g_s, g_r, w_s, w_r, f_s, f_r,
):
    c = lax.axis_index("ctx")
    h = lax.axis_index("kvh")
    shards = lax.axis_size("ctx")
    y = h // 2
    core = h % 2
    after = lax.rem(c + 1, shards)
    before = lax.rem(c + shards - 1, shards)

    def to(i):
        return lax.rem(y + i // 2, 4) * 2 + lax.rem(core + i % 2, 2)

    def source(i):
        return lax.rem(y - i // 2 + 4, 4) * 2 + lax.rem(core - i % 2 + 2, 2)

    def rows_of(p):
        return pl.ds(pl.multiple_of(p * ROWS, ROWS), ROWS)

    def wide(p):
        return pl.ds(pl.multiple_of(p * GW, GW), GW)

    def narrow(p):
        return pl.ds(pl.multiple_of(p * HD, HD), HD)

    own = [
        pltpu.make_async_copy(k_ref.at[:, narrow(h)], kw.at[pl.ds(pl.multiple_of(3 * SHARD + h * ROWS, ROWS), ROWS)], kv_r.at[0, 0]),
        pltpu.make_async_copy(v_ref.at[:, narrow(h)], vw.at[pl.ds(pl.multiple_of(3 * SHARD + h * ROWS, ROWS), ROWS)], kv_r.at[0, 1]),
        pltpu.make_async_copy(q_ref.at[:, wide(h)], qb.at[h], q_r.at[0, 0]),
        pltpu.make_async_copy(go_ref.at[:, wide(h)], gb.at[h], q_r.at[0, 1]),
    ]
    for copy in own:
        copy.start()

    barrier = pltpu.get_barrier_semaphore()
    for i in range(1, PEERS):
        pl.semaphore_signal(barrier, inc=1, device_id=(c, to(i)), device_id_type=MESH)
    pl.semaphore_signal(barrier, inc=1, device_id=(after, h), device_id_type=MESH)
    pl.semaphore_signal(barrier, inc=1, device_id=(before, h), device_id_type=MESH)
    pl.semaphore_wait(barrier, PEERS + 1)

    def remote(src, dst, send, recv, device):
        return pltpu.make_async_remote_copy(
            src_ref=src, dst_ref=dst, send_sem=send, recv_sem=recv,
            device_id=device, device_id_type=MESH,
        )

    sends = []
    mine = pl.ds(pl.multiple_of(3 * SHARD + h * ROWS, ROWS), ROWS)
    for i in range(1, PEERS):
        p = to(i)
        for n, (src, dst) in enumerate(((k_ref, kw), (v_ref, vw))):
            copy = remote(src.at[:, narrow(p)], dst.at[mine], kv_s.at[i, n], kv_r.at[i, n], (c, p))
            copy.start()
            sends.append(copy)
    for i in range(1, PEERS):
        p = to(i)
        for n, (src, dst) in enumerate(((q_ref, qb), (go_ref, gb))):
            copy = remote(src.at[:, wide(p)], dst.at[h], q_s.at[i, n], q_r.at[i, n], (c, p))
            copy.start()
            sends.append(copy)

    for i in range(PEERS):
        for n, dst in enumerate((kw, vw)):
            piece = dst.at[pl.ds(pl.multiple_of(3 * SHARD + source(i) * ROWS, ROWS), ROWS)]
            pltpu.make_async_copy(piece, piece, kv_r.at[i, n]).wait()

    def ring(step):
        out = []
        for half in range(2):
            for n, buf in enumerate((kw, vw)):
                src = buf.at[pl.ds((3 - step) * SHARD + half * 128, 128)]
                dst = buf.at[pl.ds((2 - step) * SHARD + half * 128, 128)]
                at = half * 2 + n
                out.append(remote(src, dst, z_s.at[step, at], z_r.at[step, at], (after, h)))
        return out

    def transposed(block):
        at = pl.ds(block * SHARD, SHARD)
        kt[:, at] = kw[at, :].T
        vt[:, at] = vw[at, :].T

    steps = [ring(step) for step in range(REACH)]
    for copy in steps[0]:
        copy.start()

    eye = lax.broadcasted_iota(jnp.int32, (128, 128), 0) == lax.broadcasted_iota(jnp.int32, (128, 128), 1)
    doc_rows = []
    for tile in range(8):
        row = 2 * c - 6 + tile
        line = doc_ref[pl.ds(jnp.maximum(row, 0), 1), :].astype(F32)
        line = jnp.where(row >= 0, line, -1.0)
        doc_rows.append(line)
        column = jnp.sum(jnp.where(eye, jnp.broadcast_to(line, (128, 128)), 0.0), axis=1, keepdims=True)
        kd[tile * 128 : (tile + 1) * 128, :] = jnp.broadcast_to(column, (128, 128))
    lane = lax.broadcasted_iota(jnp.int32, (1, 128), 1)
    key_row = lax.broadcasted_iota(jnp.int32, (128, 128), 0)
    for r in range(PEERS):
        start = 128 * (r // 4)
        line = jnp.where(lane // ROWS == r % 4, doc_rows[6 + r // 4], 0.0)
        line = line + pltpu.roll(line, 32, 1) + pltpu.roll(line, 64, 1) + pltpu.roll(line, 96, 1)
        position = REACH * SHARD + r * ROWS + lane % ROWS
        for tile in range(7):
            at = start + tile * 128
            seen = kd[at : at + 128, :] == line
            if at + 128 > REACH * SHARD:
                seen = seen & (key_row + at <= position)
            bias[r, tile * 128 : (tile + 1) * 128, :] = jnp.where(seen, 0.0, -1e30)

    transposed(3)
    for step in range(REACH):
        for at, copy in enumerate(steps[step]):
            copy.wait_recv()
            if step < REACH - 1:
                steps[step + 1][at].start()
        transposed(2 - step)

    def forward(i, carry):
        r = source(i)
        for n, buf in enumerate((qb, gb)):
            pltpu.make_async_copy(buf.at[r], buf.at[r], q_r.at[i, n]).wait()
        start = pl.multiple_of(128 * (r // 4), 128)
        keys = pl.ds(start, SPAN)
        lanes = pl.ds(pl.multiple_of(r * 256, 256), 256)
        q2 = jnp.concatenate([qb[r, :, j * HD : (j + 1) * HD] for j in range(8)], axis=0)
        g2 = jnp.concatenate([gb[r, :, j * HD : (j + 1) * HD] for j in range(8)], axis=0)
        qall[lanes, :] = q2
        scr[...] = dot(kw[keys, :], q2, NT)
        peak = jnp.full((8, 256), -3e38, F32)
        for tile in range(7):
            at = slice(tile * 128, (tile + 1) * 128)
            extra = bias[r, at, :]
            x = scr[at, :] * (SCALE * LOG2E) + jnp.concatenate([extra, extra], axis=1)
            scr[at, :] = x
            peak = jnp.maximum(peak, jnp.max(x.reshape(16, 8, 256), axis=0))
        peak = jnp.max(peak, axis=0, keepdims=True)
        total = jnp.zeros((8, 256), F32)
        for tile in range(7):
            e = jnp.exp2(scr[tile * 128 : (tile + 1) * 128, :] - peak)
            total = total + jnp.sum(e.reshape(16, 8, 256), axis=0)
            eall[pl.ds(start + tile * 128, 128), lanes] = e.astype(BF16)
        inverse = 1.0 / jnp.sum(total, axis=0, keepdims=True)
        o_t = dot(vt[:, keys], eall[keys, lanes]) * inverse
        o2 = o_t.T.astype(BF16)
        for j in range(8):
            ob[r, :, j * HD : (j + 1) * HD] = o2[j * ROWS : (j + 1) * ROWS, :]
        g_t = g2.astype(F32).T
        delta = jnp.sum(g_t * o_t.astype(BF16).astype(F32), axis=0, keepdims=True) * inverse
        scaled = (g_t * inverse).astype(BF16)
        got[:, lanes] = scaled
        scr[...] = dot(vw[keys, :], scaled)
        for tile in range(7):
            rows = pl.ds(start + tile * 128, 128)
            ds = eall[rows, lanes].astype(F32) * (scr[tile * 128 : (tile + 1) * 128, :] - delta)
            dsall[rows, lanes] = ds.astype(BF16)

        @pl.when(i > 0)
        def _():
            remote(ob.at[r], att_ref.at[:, wide(h)], o_s.at[i], o_r.at[i], (c, r)).start()

        @pl.when(i == 0)
        def _():
            pltpu.make_async_copy(ob.at[r], att_ref.at[:, wide(h)], o_r.at[0]).start()

        return carry

    lax.fori_loop(0, PEERS, forward, 0)

    def gradients(block):
        for sub in range(2):
            tile = 2 * block + sub
            rows = slice(tile * 128, (tile + 1) * 128)
            lo, hi = (0, 1024) if tile == 0 else (1024, 2048) if tile == 7 else (0, 2048)
            part[0, rows, :] = dot(dsall[rows, lo:hi], qall[lo:hi, :]) * SCALE
            part[1, rows, :] = dot(eall[rows, lo:hi], got[:, lo:hi], NT)

    def relay(step):
        return [
            remote(sendk.at[step, n], recvk.at[step, n], w_s.at[step, n], w_r.at[step, n], (before, h))
            for n in range(2)
        ]

    relays = [relay(step) for step in range(REACH)]
    gradients(0)
    for n in range(2):
        sendk[0, n] = part[n, 0:SHARD, :].astype(BF16)
        relays[0][n].start()
    for block in range(1, REACH + 1):
        gradients(block)

    def query_gradients(i, carry):
        r = source(i)
        keys = pl.ds(pl.multiple_of(128 * (r // 4), 128), SPAN)
        lanes = pl.ds(pl.multiple_of(r * 256, 256), 256)
        dq = (dot(kt[:, keys], dsall[keys, lanes]) * SCALE).T.astype(BF16)
        for j in range(8):
            gqb[r, :, j * HD : (j + 1) * HD] = dq[j * ROWS : (j + 1) * ROWS, :]

        @pl.when(i > 0)
        def _():
            remote(gqb.at[r], gq_ref.at[:, wide(h)], g_s.at[i], g_r.at[i], (c, r)).start()

        @pl.when(i == 0)
        def _():
            pltpu.make_async_copy(gqb.at[r], gq_ref.at[:, wide(h)], g_r.at[0]).start()

        return carry

    lax.fori_loop(0, PEERS, query_gradients, 0)
    for step in range(REACH):
        block = slice((step + 1) * SHARD, (step + 2) * SHARD)
        for n in range(2):
            relays[step][n].wait_recv()
            total = recvk[step, n].astype(F32) + part[n, block, :]
            if step < REACH - 1:
                sendk[step + 1, n] = total.astype(BF16)
                relays[step + 1][n].start()
            else:
                fin[n] = total.astype(BF16)
    last = []
    for n, out in enumerate((gk_ref, gv_ref)):
        copy = pltpu.make_async_copy(fin.at[n, rows_of(h)], out.at[:, narrow(h)], f_r.at[0, n])
        copy.start()
        for i in range(1, PEERS):
            p = to(i)
            copy = remote(fin.at[n, rows_of(p)], out.at[:, narrow(h)], f_s.at[i, n], f_r.at[i, n], (c, p))
            copy.start()
            last.append(copy)

    for copy in sends + last:
        copy.wait_send()
    for step in range(REACH):
        for copy in steps[step] + relays[step]:
            copy.wait_send()
    for i in range(1, PEERS):
        r = source(i)
        remote(ob.at[r], att_ref.at[:, wide(h)], o_s.at[i], o_r.at[i], (c, r)).wait_send()
        remote(gqb.at[r], gq_ref.at[:, wide(h)], g_s.at[i], g_r.at[i], (c, r)).wait_send()
    for i in range(PEERS):
        p = to(i)
        for ref, sem in ((att_ref, o_r), (gq_ref, g_r)):
            piece = ref.at[:, wide(p)]
            pltpu.make_async_copy(piece, piece, sem.at[i]).wait()
        for n, ref in enumerate((gk_ref, gv_ref)):
            piece = ref.at[:, narrow(source(i))]
            pltpu.make_async_copy(piece, piece, f_r.at[i, n]).wait()


def body(queries, keys, values, documents, grad_out):
    any_spec = pl.BlockSpec(memory_space=pl.ANY)
    dma = pltpu.SemaphoreType.DMA
    return pl.pallas_call(
        kernel,
        out_shape=(
            jax.ShapeDtypeStruct((ROWS, PEERS * GW), BF16),
            jax.ShapeDtypeStruct((ROWS, PEERS * GW), BF16),
            jax.ShapeDtypeStruct((ROWS, PEERS * HD), BF16),
            jax.ShapeDtypeStruct((ROWS, PEERS * HD), BF16),
        ),
        in_specs=[any_spec, any_spec, any_spec, pl.BlockSpec(memory_space=pltpu.VMEM), any_spec],
        out_specs=(any_spec,) * 4,
        scratch_shapes=[
            pltpu.VMEM((PEERS, ROWS, GW), BF16),
            pltpu.VMEM((PEERS, ROWS, GW), BF16),
            pltpu.VMEM((WIN, HD), BF16),
            pltpu.VMEM((WIN, HD), BF16),
            pltpu.VMEM((HD, WIN), BF16),
            pltpu.VMEM((HD, WIN), BF16),
            pltpu.VMEM((2048, HD), BF16),
            pltpu.VMEM((HD, 2048), BF16),
            pltpu.VMEM((WIN, 128), F32),
            pltpu.VMEM((PEERS, SPAN, 128), F32),
            pltpu.VMEM((SPAN, 256), F32),
            pltpu.VMEM((WIN, 2048), BF16),
            pltpu.VMEM((WIN, 2048), BF16),
            pltpu.VMEM((PEERS, ROWS, GW), BF16),
            pltpu.VMEM((PEERS, ROWS, GW), BF16),
            pltpu.VMEM((2, WIN, HD), F32),
            pltpu.VMEM((REACH, 2, SHARD, HD), BF16),
            pltpu.VMEM((REACH, 2, SHARD, HD), BF16),
            pltpu.VMEM((2, SHARD, HD), BF16),
            dma((PEERS, 2)), dma((PEERS, 2)),
            dma((PEERS, 2)), dma((PEERS, 2)),
            dma((REACH, 4)), dma((REACH, 4)),
            dma((PEERS,)), dma((PEERS,)),
            dma((PEERS,)), dma((PEERS,)),
            dma((REACH, 2)), dma((REACH, 2)),
            dma((PEERS, 2)), dma((PEERS, 2)),
        ],
        compiler_params=pltpu.CompilerParams(
            collective_id=0, has_side_effects=True, vmem_limit_bytes=48 * 1024 * 1024
        ),
    )(queries, keys, values, documents.reshape(128, 128), grad_out)


def solution(mesh):
    split = P(("ctx", "kvh"), None)
    return jax.shard_map(
        body,
        mesh=mesh,
        in_specs=(split, split, split, P(), split),
        out_specs=(split,) * 4,
        check_vma=False,
    )
```

```python
import math

import jax
import jax.numpy as jnp
from jax import lax
from jax.experimental import pallas as pl
from jax.experimental.pallas import tpu as pltpu
from jax.sharding import PartitionSpec as P

HD = 128
REACH = 3
PEERS = 8
ROWS = 32
SHARD = 256
WIN = 1024
SPAN = 800
TILE = 160
PAIR = 2
GW = 1024
SCALE = 1.0 / math.sqrt(HD)
LOG2E = 1.4426950408889634
MESH = pl.DeviceIdType.MESH
F32 = jnp.float32
BF16 = jnp.bfloat16
NT = (((1,), (1,)), ((), ()))
NN = (((1,), (0,)), ((), ()))


def dot(a, b, dims=NN):
    return lax.dot_general(a, b, dims, preferred_element_type=F32)


def kernel(
    q_ref, k_ref, v_ref, doc_ref, go_ref,
    att_ref, gq_ref, gk_ref, gv_ref,
    qb, gb, kw, vw, kt, vt, qall, got, kd, bias, ob, gqb,
    part, sendk, recvk, fin,
    q_s, q_r, kv_s, kv_r, z_s, z_r, o_s, o_r, g_s, g_r, w_s, w_r, f_s, f_r,
    *work,
):
    scr, eall, dsall = work[:PAIR], work[PAIR : PAIR + PEERS], work[PAIR + PEERS :]
    c = lax.axis_index("ctx")
    h = lax.axis_index("kvh")
    shards = lax.axis_size("ctx")
    y = h // 2
    core = h % 2
    after = lax.rem(c + 1, shards)
    before = lax.rem(c + shards - 1, shards)

    def to(i):
        return lax.rem(y + i // 2, 4) * 2 + lax.rem(core + i % 2, 2)

    def source(i):
        return lax.rem(y - i // 2 + 4, 4) * 2 + lax.rem(core - i % 2 + 2, 2)

    def rows_of(p):
        return pl.ds(pl.multiple_of(p * ROWS, ROWS), ROWS)

    def wide(p):
        return pl.ds(pl.multiple_of(p * GW, GW), GW)

    def narrow(p):
        return pl.ds(pl.multiple_of(p * HD, HD), HD)

    own = [
        pltpu.make_async_copy(k_ref.at[:, narrow(h)], kw.at[pl.ds(pl.multiple_of(3 * SHARD + h * ROWS, ROWS), ROWS)], kv_r.at[0, 0]),
        pltpu.make_async_copy(v_ref.at[:, narrow(h)], vw.at[pl.ds(pl.multiple_of(3 * SHARD + h * ROWS, ROWS), ROWS)], kv_r.at[0, 1]),
        pltpu.make_async_copy(q_ref.at[:, wide(h)], qb.at[h], q_r.at[0, 0]),
        pltpu.make_async_copy(go_ref.at[:, wide(h)], gb.at[h], q_r.at[0, 1]),
    ]
    for copy in own:
        copy.start()

    barrier = pltpu.get_barrier_semaphore()
    for i in range(1, PEERS):
        pl.semaphore_signal(barrier, inc=1, device_id=(c, to(i)), device_id_type=MESH)

    @pl.when(c < shards - 1)
    def _():
        pl.semaphore_signal(barrier, inc=1, device_id=(after, h), device_id_type=MESH)

    @pl.when(c > 0)
    def _():
        pl.semaphore_signal(barrier, inc=1, device_id=(before, h), device_id_type=MESH)

    pl.semaphore_wait(barrier, PEERS - 1 + jnp.minimum(c, 1) + jnp.minimum(shards - 1 - c, 1))

    def remote(src, dst, send, recv, device):
        return pltpu.make_async_remote_copy(
            src_ref=src, dst_ref=dst, send_sem=send, recv_sem=recv,
            device_id=device, device_id_type=MESH,
        )

    sends = []
    mine = pl.ds(pl.multiple_of(3 * SHARD + h * ROWS, ROWS), ROWS)
    for i in range(1, PEERS):
        p = to(i)
        for n, (src, dst) in enumerate(((k_ref, kw), (v_ref, vw))):
            copy = remote(src.at[:, narrow(p)], dst.at[mine], kv_s.at[i, n], kv_r.at[i, n], (c, p))
            copy.start()
            sends.append(copy)
    for i in range(1, PEERS):
        p = to(i)
        for n, (src, dst) in enumerate(((q_ref, qb), (go_ref, gb))):
            copy = remote(src.at[:, wide(p)], dst.at[h], q_s.at[i, n], q_r.at[i, n], (c, p))
            copy.start()
            sends.append(copy)

    for i in range(PEERS):
        for n, dst in enumerate((kw, vw)):
            piece = dst.at[pl.ds(pl.multiple_of(3 * SHARD + source(i) * ROWS, ROWS), ROWS)]
            pltpu.make_async_copy(piece, piece, kv_r.at[i, n]).wait()

    def ring(step):
        out = []
        for half in range(2):
            for n, buf in enumerate((kw, vw)):
                src = buf.at[pl.ds((3 - step) * SHARD + half * 128, 128)]
                dst = buf.at[pl.ds((2 - step) * SHARD + half * 128, 128)]
                at = half * 2 + n
                out.append(remote(src, dst, z_s.at[step, at], z_r.at[step, at], (after, h)))
        return out

    def transposed(block):
        at = pl.ds(block * SHARD, SHARD)
        kt[:, at] = kw[at, :].T
        vt[:, at] = vw[at, :].T

    steps = [ring(step) for step in range(REACH)]

    @pl.when(c < shards - 1)
    def _():
        for copy in steps[0]:
            copy.start()

    @pl.when(c == 0)
    def _():
        kw[0 : REACH * SHARD, :] = jnp.zeros((REACH * SHARD, HD), BF16)
        vw[0 : REACH * SHARD, :] = jnp.zeros((REACH * SHARD, HD), BF16)

    @pl.when(c == shards - 1)
    def _():
        recvk[...] = jnp.zeros(recvk.shape, BF16)

    eye = lax.broadcasted_iota(jnp.int32, (128, 128), 0) == lax.broadcasted_iota(jnp.int32, (128, 128), 1)
    doc_rows = []
    for tile in range(8):
        row = 2 * c - 6 + tile
        line = doc_ref[pl.ds(jnp.maximum(row, 0), 1), :].astype(F32)
        line = jnp.where(row >= 0, line, -1.0)
        doc_rows.append(line)
        column = jnp.sum(jnp.where(eye, jnp.broadcast_to(line, (128, 128)), 0.0), axis=1, keepdims=True)
        kd[tile * 128 : (tile + 1) * 128, :] = jnp.broadcast_to(column, (128, 128))
    lane = lax.broadcasted_iota(jnp.int32, (1, 128), 1)
    key_row = lax.broadcasted_iota(jnp.int32, (TILE, 128), 0)
    for r in range(PEERS):
        start = ROWS * r
        line = jnp.where(lane // ROWS == r % 4, doc_rows[6 + r // 4], 0.0)
        line = line + pltpu.roll(line, 32, 1) + pltpu.roll(line, 64, 1) + pltpu.roll(line, 96, 1)
        position = REACH * SHARD + r * ROWS + lane % ROWS
        for at in range(0, SPAN, TILE):
            seen = kd[start + at : start + at + TILE, :] == line
            if start + at + TILE > REACH * SHARD:
                seen = seen & (key_row + (start + at) <= position)
            bias[r, at : at + TILE, :] = jnp.where(seen, 0.0, -1e30)
    for buf in (*eall, *dsall):
        buf[...] = jnp.zeros(buf.shape, BF16)

    transposed(3)
    for step in range(REACH):
        for at, copy in enumerate(steps[step]):

            @pl.when(c > 0)
            def _(copy=copy):
                copy.wait_recv()

            if step < REACH - 1:

                @pl.when(c < shards - 1)
                def _(copy=steps[step + 1][at]):
                    copy.start()

        transposed(2 - step)

    def pieces(buf, r):
        return jnp.concatenate([buf[r, :, j * HD : (j + 1) * HD] for j in range(8)], axis=0)

    def scores(i, slot):
        r = source(i)
        keys = pl.ds(pl.multiple_of(r * ROWS, ROWS), SPAN)
        q2 = pieces(qb, r)
        qall[i * 256 : (i + 1) * 256, :] = q2
        scr[slot][...] = dot(kw[keys, :], q2, NT)

    def softmax(i, slot):
        r = source(i)
        peak = jnp.full((8, 256), -3e38, F32)
        for at in range(0, SPAN, TILE):
            extra = bias[r, at : at + TILE, :]
            x = scr[slot][at : at + TILE, :] * (SCALE * LOG2E) + jnp.concatenate([extra, extra], axis=1)
            scr[slot][at : at + TILE, :] = x
            peak = jnp.maximum(peak, jnp.max(x.reshape(TILE // 8, 8, 256), axis=0))
        peak = jnp.max(peak, axis=0, keepdims=True)
        total = jnp.zeros((8, 256), F32)
        for at in range(0, SPAN, TILE):
            e = jnp.exp2(scr[slot][at : at + TILE, :] - peak)
            total = total + jnp.sum(e.reshape(TILE // 8, 8, 256), axis=0)
            eall[i][pl.ds(pl.multiple_of(r * ROWS + at, ROWS), TILE), :] = e.astype(BF16)
        return 1.0 / jnp.sum(total, axis=0, keepdims=True)

    def attend(i, inverse):
        r = source(i)
        o_t = dot(vt[...], eall[i][...]) * inverse
        o2 = o_t.T.astype(BF16)
        for j in range(8):
            ob[i, :, j * HD : (j + 1) * HD] = o2[j * ROWS : (j + 1) * ROWS, :]
        g_t = pieces(gb, r).astype(F32).T
        delta = jnp.sum(g_t * o_t.astype(BF16).astype(F32), axis=0, keepdims=True) * inverse
        got[:, i * 256 : (i + 1) * 256] = (g_t * inverse).astype(BF16)
        return delta

    def cotangents(i, slot):
        keys = pl.ds(pl.multiple_of(source(i) * ROWS, ROWS), SPAN)
        scr[slot][...] = dot(vw[keys, :], got[:, i * 256 : (i + 1) * 256])

    def score_gradients(i, slot, delta):
        r = source(i)
        for at in range(0, SPAN, TILE):
            rows = pl.ds(pl.multiple_of(r * ROWS + at, ROWS), TILE)
            ds = eall[i][rows, :].astype(F32) * (scr[slot][at : at + TILE, :] - delta)
            dsall[i][rows, :] = ds.astype(BF16)

    def query_gradients(i):
        dq = (dot(kt[...], dsall[i][...]) * SCALE).T.astype(BF16)
        for j in range(8):
            gqb[i, :, j * HD : (j + 1) * HD] = dq[j * ROWS : (j + 1) * ROWS, :]

    def give(buf, out, send, recv, i):
        r = source(i)
        if i == 0:
            return pltpu.make_async_copy(buf.at[0], out.at[:, wide(h)], recv.at[0])
        return remote(buf.at[i], out.at[:, wide(h)], send.at[i], recv.at[i], (c, r))

    for first in range(0, PEERS, PAIR):
        group = range(first, first + PAIR)
        for i in group:
            for n, buf in enumerate((qb, gb)):
                piece = buf.at[source(i)]
                pltpu.make_async_copy(piece, piece, q_r.at[i, n]).wait()
        for i in group:
            scores(i, i % PAIR)
        inverses = [softmax(i, i % PAIR) for i in group]
        deltas = [attend(i, inverse) for i, inverse in zip(group, inverses)]
        for i in group:
            cotangents(i, i % PAIR)
        for i, delta in zip(group, deltas):
            score_gradients(i, i % PAIR, delta)
        for i in group:
            query_gradients(i)
        for i in group:
            give(ob, att_ref, o_s, o_r, i).start()
            give(gqb, gq_ref, g_s, g_r, i).start()

    def gradients(rows):
        at = slice(rows[0], rows[1])
        part[0, at, :] = dot(jnp.concatenate([buf[at, :] for buf in dsall], axis=1), qall[...]) * SCALE
        part[1, at, :] = dot(jnp.concatenate([buf[at, :] for buf in eall], axis=1), got[...], NT)

    relays = [
        [
            remote(sendk.at[step, n], recvk.at[step, n], w_s.at[step, n], w_r.at[step, n], (before, h))
            for n in range(2)
        ]
        for step in range(REACH)
    ]
    gradients((0, SHARD))
    for n in range(2):
        sendk[0, n] = part[n, 0:SHARD, :].astype(BF16)

        @pl.when(c > 0)
        def _(copy=relays[0][n]):
            copy.start()

    gradients((SHARD, WIN))
    for step in range(REACH):
        block = slice((step + 1) * SHARD, (step + 2) * SHARD)
        for n in range(2):

            @pl.when(c < shards - 1)
            def _(copy=relays[step][n]):
                copy.wait_recv()

            total = recvk[step, n].astype(F32) + part[n, block, :]
            if step < REACH - 1:
                sendk[step + 1, n] = total.astype(BF16)

                @pl.when(c > 0)
                def _(copy=relays[step + 1][n]):
                    copy.start()
            else:
                fin[n] = total.astype(BF16)
    last = []
    for n, out in enumerate((gk_ref, gv_ref)):
        copy = pltpu.make_async_copy(fin.at[n, rows_of(h)], out.at[:, narrow(h)], f_r.at[0, n])
        copy.start()
        for i in range(1, PEERS):
            p = to(i)
            copy = remote(fin.at[n, rows_of(p)], out.at[:, narrow(h)], f_s.at[i, n], f_r.at[i, n], (c, p))
            copy.start()
            last.append(copy)

    for copy in sends + last:
        copy.wait_send()

    @pl.when(c < shards - 1)
    def _():
        for step in range(REACH):
            for copy in steps[step]:
                copy.wait_send()

    @pl.when(c > 0)
    def _():
        for step in range(REACH):
            for copy in relays[step]:
                copy.wait_send()

    for i in range(1, PEERS):
        give(ob, att_ref, o_s, o_r, i).wait_send()
        give(gqb, gq_ref, g_s, g_r, i).wait_send()
    for i in range(PEERS):
        p = to(i)
        for ref, sem in ((att_ref, o_r), (gq_ref, g_r)):
            piece = ref.at[:, wide(p)]
            pltpu.make_async_copy(piece, piece, sem.at[i]).wait()
        for n, ref in enumerate((gk_ref, gv_ref)):
            piece = ref.at[:, narrow(source(i))]
            pltpu.make_async_copy(piece, piece, f_r.at[i, n]).wait()


def body(queries, keys, values, documents, grad_out):
    any_spec = pl.BlockSpec(memory_space=pl.ANY)
    dma = pltpu.SemaphoreType.DMA
    return pl.pallas_call(
        kernel,
        out_shape=(
            jax.ShapeDtypeStruct((ROWS, PEERS * GW), BF16),
            jax.ShapeDtypeStruct((ROWS, PEERS * GW), BF16),
            jax.ShapeDtypeStruct((ROWS, PEERS * HD), BF16),
            jax.ShapeDtypeStruct((ROWS, PEERS * HD), BF16),
        ),
        in_specs=[any_spec, any_spec, any_spec, pl.BlockSpec(memory_space=pltpu.VMEM), any_spec],
        out_specs=(any_spec,) * 4,
        scratch_shapes=[
            pltpu.VMEM((PEERS, ROWS, GW), BF16),
            pltpu.VMEM((PEERS, ROWS, GW), BF16),
            pltpu.VMEM((WIN, HD), BF16),
            pltpu.VMEM((WIN, HD), BF16),
            pltpu.VMEM((HD, WIN), BF16),
            pltpu.VMEM((HD, WIN), BF16),
            pltpu.VMEM((2048, HD), BF16),
            pltpu.VMEM((HD, 2048), BF16),
            pltpu.VMEM((WIN, 128), F32),
            pltpu.VMEM((PEERS, SPAN, 128), F32),
            pltpu.VMEM((PEERS, ROWS, GW), BF16),
            pltpu.VMEM((PEERS, ROWS, GW), BF16),
            pltpu.VMEM((2, WIN, HD), F32),
            pltpu.VMEM((REACH, 2, SHARD, HD), BF16),
            pltpu.VMEM((REACH, 2, SHARD, HD), BF16),
            pltpu.VMEM((2, SHARD, HD), BF16),
            dma((PEERS, 2)), dma((PEERS, 2)),
            dma((PEERS, 2)), dma((PEERS, 2)),
            dma((REACH, 4)), dma((REACH, 4)),
            dma((PEERS,)), dma((PEERS,)),
            dma((PEERS,)), dma((PEERS,)),
            dma((REACH, 2)), dma((REACH, 2)),
            dma((PEERS, 2)), dma((PEERS, 2)),
            *[pltpu.VMEM((SPAN, 256), F32)] * PAIR,
            *[pltpu.VMEM((WIN, 256), BF16)] * (2 * PEERS),
        ],
        compiler_params=pltpu.CompilerParams(
            collective_id=0, has_side_effects=True, vmem_limit_bytes=67043328
        ),
    )(queries, keys, values, documents.reshape(128, 128), grad_out)


def solution(mesh):
    split = P(("ctx", "kvh"), None)
    return jax.shard_map(
        body,
        mesh=mesh,
        in_specs=(split, split, split, P(), split),
        out_specs=(split,) * 4,
        check_vma=False,
    )
```

```python
import math

import jax
import jax.numpy as jnp
from jax import lax
from jax.experimental import pallas as pl
from jax.experimental.pallas import tpu as pltpu
from jax.sharding import PartitionSpec as P

HD = 128
REACH = 3
PEERS = 8
ROWS = 32
SHARD = 256
WIN = 1024
TILE = 128
PAIR = 2
GW = 1024
SCALE = 1.0 / math.sqrt(HD)
LOG2E = 1.4426950408889634
MESH = pl.DeviceIdType.MESH
F32 = jnp.float32
BF16 = jnp.bfloat16
NT = (((1,), (1,)), ((), ()))
NN = (((1,), (0,)), ((), ()))


def dot(a, b, dims=NN):
    return lax.dot_general(a, b, dims, preferred_element_type=F32)


def kernel(
    q_ref, k_ref, v_ref, doc_ref, go_ref,
    att_ref, gq_ref, gk_ref, gv_ref,
    qb, gb, kw, vw, kt, vt, qall, gotf, gotn, kd, bias, ob, gqb, near, gts, stats,
    part, sendk, recvk, fin,
    q_s, q_r, kv_s, kv_r, z_s, z_r, o_s, o_r, g_s, g_r, w_s, w_r, f_s, f_r,
    *work,
):
    scr, eall, dsall = work[: 2 * PAIR], work[2 * PAIR : 2 * PAIR + PEERS], work[2 * PAIR + PEERS :]
    c = lax.axis_index("ctx")
    h = lax.axis_index("kvh")
    shards = lax.axis_size("ctx")
    y = h // 2
    core = h % 2
    after = lax.rem(c + 1, shards)
    before = lax.rem(c + shards - 1, shards)

    def to(i):
        return lax.rem(y + i // 2, 4) * 2 + lax.rem(core + i % 2, 2)

    def source(i):
        return lax.rem(y - i // 2 + 4, 4) * 2 + lax.rem(core - i % 2 + 2, 2)

    def rows_of(p):
        return pl.ds(pl.multiple_of(p * ROWS, ROWS), ROWS)

    def wide(p):
        return pl.ds(pl.multiple_of(p * GW, GW), GW)

    def narrow(p):
        return pl.ds(pl.multiple_of(p * HD, HD), HD)

    own = [
        pltpu.make_async_copy(k_ref.at[:, narrow(h)], kw.at[pl.ds(pl.multiple_of(3 * SHARD + h * ROWS, ROWS), ROWS)], kv_r.at[0, 0]),
        pltpu.make_async_copy(v_ref.at[:, narrow(h)], vw.at[pl.ds(pl.multiple_of(3 * SHARD + h * ROWS, ROWS), ROWS)], kv_r.at[0, 1]),
        pltpu.make_async_copy(q_ref.at[:, wide(h)], qb.at[h], q_r.at[0, 0]),
        pltpu.make_async_copy(go_ref.at[:, wide(h)], gb.at[h], q_r.at[0, 1]),
    ]
    for copy in own:
        copy.start()

    barrier = pltpu.get_barrier_semaphore()
    for i in range(1, PEERS):
        pl.semaphore_signal(barrier, inc=1, device_id=(c, to(i)), device_id_type=MESH)

    @pl.when(c < shards - 1)
    def _():
        pl.semaphore_signal(barrier, inc=1, device_id=(after, h), device_id_type=MESH)

    @pl.when(c > 0)
    def _():
        pl.semaphore_signal(barrier, inc=1, device_id=(before, h), device_id_type=MESH)

    pl.semaphore_wait(barrier, PEERS - 1 + jnp.minimum(c, 1) + jnp.minimum(shards - 1 - c, 1))

    def remote(src, dst, send, recv, device):
        return pltpu.make_async_remote_copy(
            src_ref=src, dst_ref=dst, send_sem=send, recv_sem=recv,
            device_id=device, device_id_type=MESH,
        )

    sends = []
    mine = pl.ds(pl.multiple_of(3 * SHARD + h * ROWS, ROWS), ROWS)
    for i in range(1, PEERS):
        p = to(i)
        for n, (src, dst) in enumerate(((k_ref, kw), (v_ref, vw))):
            copy = remote(src.at[:, narrow(p)], dst.at[mine], kv_s.at[i, n], kv_r.at[i, n], (c, p))
            copy.start()
            sends.append(copy)
    for i in range(1, PEERS):
        p = to(i)
        for n, (src, dst) in enumerate(((q_ref, qb), (go_ref, gb))):
            copy = remote(src.at[:, wide(p)], dst.at[h], q_s.at[i, n], q_r.at[i, n], (c, p))
            copy.start()
            sends.append(copy)

    for i in range(PEERS):
        for n, dst in enumerate((kw, vw)):
            piece = dst.at[pl.ds(pl.multiple_of(3 * SHARD + source(i) * ROWS, ROWS), ROWS)]
            pltpu.make_async_copy(piece, piece, kv_r.at[i, n]).wait()

    def ring(step):
        out = []
        for half in range(2):
            for n, buf in enumerate((kw, vw)):
                src = buf.at[pl.ds((3 - step) * SHARD + half * 128, 128)]
                dst = buf.at[pl.ds((2 - step) * SHARD + half * 128, 128)]
                at = half * 2 + n
                out.append(remote(src, dst, z_s.at[step, at], z_r.at[step, at], (after, h)))
        return out

    def transposed(block):
        at = pl.ds(block * SHARD, SHARD)
        kt[:, at] = kw[at, :].T
        vt[:, at] = vw[at, :].T

    steps = [ring(step) for step in range(REACH)]

    @pl.when(c < shards - 1)
    def _():
        for copy in steps[0]:
            copy.start()

    @pl.when(c == 0)
    def _():
        kw[0 : REACH * SHARD, :] = jnp.zeros((REACH * SHARD, HD), BF16)
        vw[0 : REACH * SHARD, :] = jnp.zeros((REACH * SHARD, HD), BF16)

    @pl.when(c == shards - 1)
    def _():
        recvk[...] = jnp.zeros(recvk.shape, BF16)

    eye = lax.broadcasted_iota(jnp.int32, (128, 128), 0) == lax.broadcasted_iota(jnp.int32, (128, 128), 1)
    doc_rows = []
    for tile in range(8):
        row = 2 * c - 6 + tile
        line = doc_ref[pl.ds(jnp.maximum(row, 0), 1), :].astype(F32)
        line = jnp.where(row >= 0, line, -1.0)
        doc_rows.append(line)
        column = jnp.sum(jnp.where(eye, jnp.broadcast_to(line, (128, 128)), 0.0), axis=1, keepdims=True)
        kd[tile * 128 : (tile + 1) * 128, :] = jnp.broadcast_to(column, (128, 128))
    lane = lax.broadcasted_iota(jnp.int32, (1, 128), 1)
    key_row = lax.broadcasted_iota(jnp.int32, (TILE, 128), 0)
    for r in range(PEERS):
        line = jnp.where(lane // ROWS == r % 4, doc_rows[6 + r // 4], 0.0)
        line = line + pltpu.roll(line, 32, 1) + pltpu.roll(line, 64, 1) + pltpu.roll(line, 96, 1)
        position = REACH * SHARD + r * ROWS + lane % ROWS
        for at in range(0, WIN, TILE):
            seen = kd[at : at + TILE, :] == line
            if at >= REACH * SHARD:
                seen = seen & (key_row + at <= position)
            bias[r, at : at + TILE, :] = jnp.where(seen, 0.0, -1e30)

    def arrive(step):
        for at, copy in enumerate(steps[step]):

            @pl.when(c > 0)
            def _(copy=copy):
                copy.wait_recv()

            if step < REACH - 1:

                @pl.when(c < shards - 1)
                def _(copy=steps[step + 1][at]):
                    copy.start()

        transposed(2 - step)

    transposed(3)
    arrive(0)
    arrive(1)

    def pieces(buf, r):
        return jnp.concatenate([buf[r, :, j * HD : (j + 1) * HD] for j in range(8)], axis=0)

    def softmax(i, slot, lo, hi):
        r = source(i)
        scr[slot][lo:hi, :] = dot(kw[lo:hi, :], qall[i * 256 : (i + 1) * 256, :], NT)
        peak = jnp.full((8, 256), -3e38, F32)
        for at in range(lo, hi, TILE):
            extra = bias[r, at : at + TILE, :]
            x = scr[slot][at : at + TILE, :] * (SCALE * LOG2E) + jnp.concatenate([extra, extra], axis=1)
            scr[slot][at : at + TILE, :] = x
            peak = jnp.maximum(peak, jnp.max(x.reshape(TILE // 8, 8, 256), axis=0))
        peak = jnp.max(peak, axis=0, keepdims=True)
        total = jnp.zeros((8, 256), F32)
        for at in range(lo, hi, TILE):
            e = jnp.exp2(scr[slot][at : at + TILE, :] - peak)
            total = total + jnp.sum(e.reshape(TILE // 8, 8, 256), axis=0)
            eall[i][at : at + TILE, :] = e.astype(BF16)
        return peak, jnp.sum(total, axis=0, keepdims=True), dot(vt[:, lo:hi], eall[i][lo:hi, :])

    def ahead(i, slot):
        r = source(i)
        qall[i * 256 : (i + 1) * 256, :] = pieces(qb, r)
        gts[i] = pieces(gb, r).astype(F32).T
        peak, total, term = softmax(i, slot, SHARD, WIN)
        near[i] = term
        stats[i, 0:1, :] = peak
        stats[i, 1:2, :] = total

    def attend(i, slot):
        far_peak, far_total, term = softmax(i, slot, 0, SHARD)
        peak = jnp.maximum(far_peak, stats[i, 0:1, :])
        far = jnp.exp2(far_peak - peak)
        close = jnp.exp2(stats[i, 0:1, :] - peak)
        inverse = 1.0 / (far_total * far + stats[i, 1:2, :] * close)
        far = far * inverse
        close = close * inverse
        o_t = (term * far + near[i] * close).astype(BF16).astype(F32)
        o2 = o_t.T.astype(BF16)
        for j in range(8):
            ob[i, :, j * HD : (j + 1) * HD] = o2[j * ROWS : (j + 1) * ROWS, :]
        g_t = gts[i]
        delta = jnp.sum(g_t * o_t, axis=0, keepdims=True)
        gotf[:, i * 256 : (i + 1) * 256] = (g_t * far).astype(BF16)
        gotn[:, i * 256 : (i + 1) * 256] = (g_t * close).astype(BF16)
        return delta * far, delta * close

    ranges = ((0, SHARD, gotf), (SHARD, WIN, gotn))

    def cotangents(i, slot):
        for lo, hi, got in ranges:
            scr[slot][lo:hi, :] = dot(vw[lo:hi, :], got[:, i * 256 : (i + 1) * 256])

    def score_gradients(i, slot, deltas):
        for (lo, hi, _), delta in zip(ranges, deltas):
            for at in range(lo, hi, TILE):
                rows = slice(at, at + TILE)
                dsall[i][rows, :] = (eall[i][rows, :].astype(F32) * (scr[slot][rows, :] - delta)).astype(BF16)

    def query_gradients(i):
        dq = (dot(kt[...], dsall[i][...]) * SCALE).T.astype(BF16)
        for j in range(8):
            gqb[i, :, j * HD : (j + 1) * HD] = dq[j * ROWS : (j + 1) * ROWS, :]

    def give(buf, out, send, recv, i):
        r = source(i)
        if i == 0:
            return pltpu.make_async_copy(buf.at[0], out.at[:, wide(h)], recv.at[0])
        return remote(buf.at[i], out.at[:, wide(h)], send.at[i], recv.at[i], (c, r))

    def begin(first):
        group = range(first, first + PAIR)
        for i in group:
            for n, buf in enumerate((qb, gb)):
                piece = buf.at[source(i)]
                pltpu.make_async_copy(piece, piece, q_r.at[i, n]).wait()

    def early(first):
        return [attend(i, i % PAIR) for i in range(first, first + PAIR)]

    def late(first, deltas):
        group = range(first, first + PAIR)
        for i in group:
            cotangents(i, PAIR + i % PAIR)
        for i, delta in zip(group, deltas):
            score_gradients(i, PAIR + i % PAIR, delta)
        for i in group:
            query_gradients(i)

    pairs = (0, 2, 6, 4)
    split = 3

    def prepare(place):
        begin(pairs[place])
        for i in range(pairs[place], pairs[place] + PAIR):
            ahead(i, place % 2 * PAIR + i % PAIR)

    for place in range(split):
        prepare(place)
    arrive(2)
    deltas = early(pairs[0])
    for place in range(1, len(pairs)):
        before_it = pairs[place - 1]
        for i in range(before_it, before_it + PAIR):
            give(ob, att_ref, o_s, o_r, i).start()
        if place + split - 1 < len(pairs):
            prepare(place + split - 1)
        late(before_it, deltas)
        deltas = early(pairs[place])
        for i in range(before_it, before_it + PAIR):
            give(gqb, gq_ref, g_s, g_r, i).start()
    final = pairs[-1]
    for i in range(final, final + PAIR):
        give(ob, att_ref, o_s, o_r, i).start()
    late(final, deltas)

    def gradients(n, lo, hi):
        at = slice(lo, hi)
        if n == 0:
            part[0, at, :] = dot(jnp.concatenate([buf[at, :] for buf in dsall], axis=1), qall[...]) * SCALE
        else:
            got = gotf if hi == SHARD else gotn
            part[1, at, :] = dot(jnp.concatenate([buf[at, :] for buf in eall], axis=1), got[...], NT)

    halves = [(n, pl.ds(half * 128, 128), half * 2 + n) for half in range(2) for n in (1, 0)]
    relays = [
        [
            remote(sendk.at[step, n, at], recvk.at[step, n, at], w_s.at[step, place], w_r.at[step, place], (before, h))
            for n, at, place in halves
        ]
        for step in range(REACH)
    ]
    gradients(1, 0, SHARD)
    gradients(0, 0, SHARD)
    for (n, at, place), copy in zip(halves, relays[0]):
        sendk[0, n, at] = part[n, at, :].astype(BF16)

        @pl.when(c > 0)
        def _(copy=copy):
            copy.start()

    for i in range(final, final + PAIR):
        give(gqb, gq_ref, g_s, g_r, i).start()
    gradients(1, SHARD, WIN)
    gradients(0, SHARD, WIN)
    for copy in sends:
        copy.wait_send()

    @pl.when(c < shards - 1)
    def _():
        for step in range(REACH):
            for copy in steps[step]:
                copy.wait_send()

    last = []
    for step in range(REACH):
        for spot, (n, at, place) in enumerate(halves):

            @pl.when(c < shards - 1)
            def _(copy=relays[step][spot]):
                copy.wait_recv()

            mine = pl.ds((step + 1) * SHARD + at.start, 128)
            total = (recvk[step, n, at].astype(F32) + part[n, mine, :]).astype(BF16)
            if step < REACH - 1:
                sendk[step + 1, n, at] = total

                @pl.when(c > 0)
                def _(copy=relays[step + 1][spot]):
                    copy.start()
            else:
                fin[n, at] = total
    outs = (gk_ref, gv_ref)
    for n, out in enumerate(outs):
        copy = pltpu.make_async_copy(fin.at[n, rows_of(h)], out.at[:, narrow(h)], f_r.at[0, n])
        copy.start()
        for i in range(1, PEERS):
            p = to(i)
            copy = remote(fin.at[n, rows_of(p)], out.at[:, narrow(h)], f_s.at[i, n], f_r.at[i, n], (c, p))
            copy.start()
            last.append(copy)

    @pl.when(c > 0)
    def _():
        for step in range(REACH):
            for copy in relays[step]:
                copy.wait_send()

    for i in range(1, PEERS):
        give(ob, att_ref, o_s, o_r, i).wait_send()
        give(gqb, gq_ref, g_s, g_r, i).wait_send()
    for i in range(PEERS):
        for ref, sem in ((att_ref, o_r), (gq_ref, g_r)):
            piece = ref.at[:, wide(to(i))]
            pltpu.make_async_copy(piece, piece, sem.at[i]).wait()
    for copy in last:
        copy.wait_send()
    for i in range(PEERS):
        for n, ref in enumerate(outs):
            piece = ref.at[:, narrow(source(i))]
            pltpu.make_async_copy(piece, piece, f_r.at[i, n]).wait()


def finish(*refs):
    sources, outs, held, sem = refs[:4], refs[4:8], refs[8:12], refs[12]
    into = [pltpu.make_async_copy(sources[n], held[n], sem.at[0, n]) for n in range(4)]
    back = [pltpu.make_async_copy(held[n], outs[n], sem.at[1, n]) for n in range(4)]
    for copy in into:
        copy.start()
    for arrived, copy in zip(into, back):
        arrived.wait()
        copy.start()
    for copy in back:
        copy.wait()


def body(queries, keys, values, documents, grad_out):
    held = pl.BlockSpec(memory_space=pltpu.HBM)
    dma = pltpu.SemaphoreType.DMA
    parts = pl.pallas_call(
        kernel,
        out_shape=(
            jax.ShapeDtypeStruct((ROWS, PEERS * GW), BF16),
            jax.ShapeDtypeStruct((ROWS, PEERS * GW), BF16),
            jax.ShapeDtypeStruct((ROWS, PEERS * HD), BF16),
            jax.ShapeDtypeStruct((ROWS, PEERS * HD), BF16),
        ),
        in_specs=[held, held, held, pl.BlockSpec(memory_space=pltpu.VMEM), held],
        out_specs=(held,) * 4,
        scratch_shapes=[
            pltpu.VMEM((PEERS, ROWS, GW), BF16),
            pltpu.VMEM((PEERS, ROWS, GW), BF16),
            pltpu.VMEM((WIN, HD), BF16),
            pltpu.VMEM((WIN, HD), BF16),
            pltpu.VMEM((HD, WIN), BF16),
            pltpu.VMEM((HD, WIN), BF16),
            pltpu.VMEM((2048, HD), BF16),
            pltpu.VMEM((HD, 2048), BF16),
            pltpu.VMEM((HD, 2048), BF16),
            pltpu.VMEM((WIN, 128), F32),
            pltpu.VMEM((PEERS, WIN, 128), F32),
            pltpu.VMEM((PEERS, ROWS, GW), BF16),
            pltpu.VMEM((PEERS, ROWS, GW), BF16),
            pltpu.VMEM((PEERS, HD, 256), F32),
            pltpu.VMEM((PEERS, HD, 256), F32),
            pltpu.VMEM((PEERS, 8, 256), F32),
            pltpu.VMEM((2, WIN, HD), F32),
            pltpu.VMEM((REACH, 2, SHARD, HD), BF16),
            pltpu.VMEM((REACH, 2, SHARD, HD), BF16),
            pltpu.VMEM((2, SHARD, HD), BF16),
            dma((PEERS, 2)), dma((PEERS, 2)),
            dma((PEERS, 2)), dma((PEERS, 2)),
            dma((REACH, 4)), dma((REACH, 4)),
            dma((PEERS,)), dma((PEERS,)),
            dma((PEERS,)), dma((PEERS,)),
            dma((REACH, 4)), dma((REACH, 4)),
            dma((PEERS, 2)), dma((PEERS, 2)),
            *[pltpu.VMEM((WIN, 256), F32)] * (2 * PAIR),
            *[pltpu.VMEM((WIN, 256), BF16)] * (2 * PEERS),
        ],
        compiler_params=pltpu.CompilerParams(
            collective_id=0, has_side_effects=True, vmem_limit_bytes=67043328
        ),
    )(queries, keys, values, documents.reshape(128, 128), grad_out)
    return pl.pallas_call(
        finish,
        out_shape=[jax.ShapeDtypeStruct(part.shape, BF16) for part in parts],
        in_specs=[held] * 4,
        out_specs=[held] * 4,
        scratch_shapes=[pltpu.VMEM(part.shape, BF16) for part in parts] + [dma((2, 4))],
    )(*parts)


def solution(mesh):
    split = P(("ctx", "kvh"), None)
    return jax.shard_map(
        body,
        mesh=mesh,
        in_specs=(split, split, split, P(), split),
        out_specs=(split,) * 4,
        check_vma=False,
    )
```

```python
import math

import jax
import jax.numpy as jnp
from jax import lax
from jax.experimental import pallas as pl
from jax.experimental.pallas import tpu as pltpu
from jax.sharding import PartitionSpec as P

HD = 128
REACH = 3
PEERS = 8
ROWS = 32
SHARD = 256
WIN = 1024
TILE = 128
PAIR = 2
GW = 1024
SCALE = 1.0 / math.sqrt(HD)
LOG2E = 1.4426950408889634
MESH = pl.DeviceIdType.MESH
F32 = jnp.float32
BF16 = jnp.bfloat16
NT = (((1,), (1,)), ((), ()))
NN = (((1,), (0,)), ((), ()))


def dot(a, b, dims=NN):
    return lax.dot_general(a, b, dims, preferred_element_type=F32)


def kernel(
    q_ref, k_ref, v_ref, doc_ref, go_ref,
    att_ref, gq_ref, gk_ref, gv_ref,
    qb, gb, kw, vw, kt, vt, qall, gotf, gotn, kd, bias, ob, gqb, near, gts, stats,
    part, sendk, recvk, fin,
    q_s, q_r, kv_s, kv_r, z_s, z_r, o_s, o_r, g_s, g_r, w_s, w_r, f_s, f_r,
    *work,
):
    scr, eall, dsall = work[: 2 * PAIR], work[2 * PAIR : 2 * PAIR + PEERS], work[2 * PAIR + PEERS :]
    c = lax.axis_index("ctx")
    h = lax.axis_index("kvh")
    shards = lax.axis_size("ctx")
    y = h // 2
    core = h % 2
    after = lax.rem(c + 1, shards)
    before = lax.rem(c + shards - 1, shards)

    def to(i):
        return lax.rem(y + i // 2, 4) * 2 + lax.rem(core + i % 2, 2)

    def source(i):
        return lax.rem(y - i // 2 + 4, 4) * 2 + lax.rem(core - i % 2 + 2, 2)

    def rows_of(p):
        return pl.ds(pl.multiple_of(p * ROWS, ROWS), ROWS)

    def wide(p):
        return pl.ds(pl.multiple_of(p * GW, GW), GW)

    def narrow(p):
        return pl.ds(pl.multiple_of(p * HD, HD), HD)

    own = [
        pltpu.make_async_copy(k_ref.at[:, narrow(h)], kw.at[pl.ds(pl.multiple_of(3 * SHARD + h * ROWS, ROWS), ROWS)], kv_r.at[0, 0]),
        pltpu.make_async_copy(v_ref.at[:, narrow(h)], vw.at[pl.ds(pl.multiple_of(3 * SHARD + h * ROWS, ROWS), ROWS)], kv_r.at[0, 1]),
        pltpu.make_async_copy(q_ref.at[:, wide(h)], qb.at[h], q_r.at[0, 0]),
        pltpu.make_async_copy(go_ref.at[:, wide(h)], gb.at[h], q_r.at[0, 1]),
    ]
    for copy in own:
        copy.start()

    barrier = pltpu.get_barrier_semaphore()
    for i in range(1, PEERS):
        pl.semaphore_signal(barrier, inc=1, device_id=(c, to(i)), device_id_type=MESH)

    @pl.when(c < shards - 1)
    def _():
        pl.semaphore_signal(barrier, inc=1, device_id=(after, h), device_id_type=MESH)

    @pl.when(c > 0)
    def _():
        pl.semaphore_signal(barrier, inc=1, device_id=(before, h), device_id_type=MESH)

    pl.semaphore_wait(barrier, PEERS - 1 + jnp.minimum(c, 1) + jnp.minimum(shards - 1 - c, 1))

    def remote(src, dst, send, recv, device):
        return pltpu.make_async_remote_copy(
            src_ref=src, dst_ref=dst, send_sem=send, recv_sem=recv,
            device_id=device, device_id_type=MESH,
        )

    sends = []
    mine = pl.ds(pl.multiple_of(3 * SHARD + h * ROWS, ROWS), ROWS)
    for i in range(1, PEERS):
        p = to(i)
        for n, (src, dst) in enumerate(((k_ref, kw), (v_ref, vw))):
            copy = remote(src.at[:, narrow(p)], dst.at[mine], kv_s.at[i, n], kv_r.at[i, n], (c, p))
            copy.start()
            sends.append(copy)
    for i in range(1, PEERS):
        p = to(i)
        for n, (src, dst) in enumerate(((q_ref, qb), (go_ref, gb))):
            copy = remote(src.at[:, wide(p)], dst.at[h], q_s.at[i, n], q_r.at[i, n], (c, p))
            copy.start()
            sends.append(copy)

    def rows_in(block, i):
        return pl.ds(pl.multiple_of(block * SHARD + source(i) * ROWS, ROWS), ROWS)

    def ring(step):
        out = []
        for i in range(PEERS):
            for n, buf in enumerate((kw, vw)):
                src, dst = buf.at[rows_in(3 - step, i)], buf.at[rows_in(2 - step, i)]
                at = i * 2 + n
                out.append(remote(src, dst, z_s.at[step, at], z_r.at[step, at], (after, h)))
        return out

    steps = [ring(step) for step in range(REACH)]
    for i in range(PEERS):
        for n, dst in enumerate((kw, vw)):
            piece = dst.at[rows_in(3, i)]
            pltpu.make_async_copy(piece, piece, kv_r.at[i, n]).wait()

        @pl.when(c < shards - 1)
        def _(copies=steps[0][2 * i : 2 * i + 2]):
            for copy in copies:
                copy.start()

    def transposed(block):
        at = pl.ds(block * SHARD, SHARD)
        kt[:, at] = kw[at, :].T
        vt[:, at] = vw[at, :].T

    @pl.when(c == 0)
    def _():
        kw[0 : REACH * SHARD, :] = jnp.zeros((REACH * SHARD, HD), BF16)
        vw[0 : REACH * SHARD, :] = jnp.zeros((REACH * SHARD, HD), BF16)

    @pl.when(c == shards - 1)
    def _():
        recvk[...] = jnp.zeros(recvk.shape, BF16)

    eye = lax.broadcasted_iota(jnp.int32, (128, 128), 0) == lax.broadcasted_iota(jnp.int32, (128, 128), 1)
    doc_rows = []
    for tile in range(8):
        row = 2 * c - 6 + tile
        line = doc_ref[pl.ds(jnp.maximum(row, 0), 1), :].astype(F32)
        line = jnp.where(row >= 0, line, -1.0)
        doc_rows.append(line)
        column = jnp.sum(jnp.where(eye, jnp.broadcast_to(line, (128, 128)), 0.0), axis=1, keepdims=True)
        kd[tile * 128 : (tile + 1) * 128, :] = jnp.broadcast_to(column, (128, 128))
    lane = lax.broadcasted_iota(jnp.int32, (1, 128), 1)
    key_row = lax.broadcasted_iota(jnp.int32, (TILE, 128), 0)
    for r in range(PEERS):
        line = jnp.where(lane // ROWS == r % 4, doc_rows[6 + r // 4], 0.0)
        line = line + pltpu.roll(line, 32, 1) + pltpu.roll(line, 64, 1) + pltpu.roll(line, 96, 1)
        position = REACH * SHARD + r * ROWS + lane % ROWS
        for at in range(0, WIN, TILE):
            seen = kd[at : at + TILE, :] == line
            if at >= REACH * SHARD:
                seen = seen & (key_row + at <= position)
            bias[r, at : at + TILE, :] = jnp.where(seen, 0.0, -1e30)

    def arrive(step):
        for i in range(PEERS):

            @pl.when(c > 0)
            def _(copies=steps[step][2 * i : 2 * i + 2]):
                for copy in copies:
                    copy.wait_recv()

            if step < REACH - 1:

                @pl.when(c < shards - 1)
                def _(copies=steps[step + 1][2 * i : 2 * i + 2]):
                    for copy in copies:
                        copy.start()

        transposed(2 - step)

    transposed(3)
    arrive(0)
    arrive(1)

    def pieces(buf, r):
        return jnp.concatenate([buf[r, :, j * HD : (j + 1) * HD] for j in range(8)], axis=0)

    def softmax(i, slot, lo, hi):
        r = source(i)
        scr[slot][lo:hi, :] = dot(kw[lo:hi, :], qall[i * 256 : (i + 1) * 256, :], NT)
        peak = jnp.full((8, 256), -3e38, F32)
        for at in range(lo, hi, TILE):
            extra = bias[r, at : at + TILE, :]
            x = scr[slot][at : at + TILE, :] * (SCALE * LOG2E) + jnp.concatenate([extra, extra], axis=1)
            scr[slot][at : at + TILE, :] = x
            peak = jnp.maximum(peak, jnp.max(x.reshape(TILE // 8, 8, 256), axis=0))
        peak = jnp.max(peak, axis=0, keepdims=True)
        total = jnp.zeros((8, 256), F32)
        for at in range(lo, hi, TILE):
            e = jnp.exp2(scr[slot][at : at + TILE, :] - peak)
            total = total + jnp.sum(e.reshape(TILE // 8, 8, 256), axis=0)
            eall[i][at : at + TILE, :] = e.astype(BF16)
        return peak, jnp.sum(total, axis=0, keepdims=True), dot(vt[:, lo:hi], eall[i][lo:hi, :])

    def ahead(i, slot):
        r = source(i)
        qall[i * 256 : (i + 1) * 256, :] = pieces(qb, r)
        gts[i] = pieces(gb, r).astype(F32).T
        peak, total, term = softmax(i, slot, SHARD, WIN)
        near[i] = term
        stats[i, 0:1, :] = peak
        stats[i, 1:2, :] = total

    def attend(i, slot):
        far_peak, far_total, term = softmax(i, slot, 0, SHARD)
        peak = jnp.maximum(far_peak, stats[i, 0:1, :])
        far = jnp.exp2(far_peak - peak)
        close = jnp.exp2(stats[i, 0:1, :] - peak)
        inverse = 1.0 / (far_total * far + stats[i, 1:2, :] * close)
        far = far * inverse
        close = close * inverse
        o_t = (term * far + near[i] * close).astype(BF16).astype(F32)
        o2 = o_t.T.astype(BF16)
        for j in range(8):
            ob[i, :, j * HD : (j + 1) * HD] = o2[j * ROWS : (j + 1) * ROWS, :]
        g_t = gts[i]
        delta = jnp.sum(g_t * o_t, axis=0, keepdims=True)
        gotf[:, i * 256 : (i + 1) * 256] = (g_t * far).astype(BF16)
        gotn[:, i * 256 : (i + 1) * 256] = (g_t * close).astype(BF16)
        return delta * far, delta * close

    ranges = ((0, SHARD, gotf), (SHARD, WIN, gotn))

    def cotangents(i, slot):
        for lo, hi, got in ranges:
            scr[slot][lo:hi, :] = dot(vw[lo:hi, :], got[:, i * 256 : (i + 1) * 256])

    def score_gradients(i, slot, deltas):
        for (lo, hi, _), delta in zip(ranges, deltas):
            for at in range(lo, hi, TILE):
                rows = slice(at, at + TILE)
                dsall[i][rows, :] = (eall[i][rows, :].astype(F32) * (scr[slot][rows, :] - delta)).astype(BF16)

    def query_gradients(i):
        dq = (dot(kt[...], dsall[i][...]) * SCALE).T.astype(BF16)
        for j in range(8):
            gqb[i, :, j * HD : (j + 1) * HD] = dq[j * ROWS : (j + 1) * ROWS, :]

    def give(buf, out, send, recv, i):
        r = source(i)
        if i == 0:
            return pltpu.make_async_copy(buf.at[0], out.at[:, wide(h)], recv.at[0])
        return remote(buf.at[i], out.at[:, wide(h)], send.at[i], recv.at[i], (c, r))

    def begin(first):
        group = range(first, first + PAIR)
        for i in group:
            for n, buf in enumerate((qb, gb)):
                piece = buf.at[source(i)]
                pltpu.make_async_copy(piece, piece, q_r.at[i, n]).wait()

    def early(first):
        return [attend(i, i % PAIR) for i in range(first, first + PAIR)]

    def late(first, deltas):
        group = range(first, first + PAIR)
        for i in group:
            cotangents(i, PAIR + i % PAIR)
        for i, delta in zip(group, deltas):
            score_gradients(i, PAIR + i % PAIR, delta)
        for i in group:
            query_gradients(i)

    pairs = (0, 2, 6, 4)
    split = 3

    def prepare(place):
        begin(pairs[place])
        for i in range(pairs[place], pairs[place] + PAIR):
            ahead(i, place % 2 * PAIR + i % PAIR)

    for place in range(split):
        prepare(place)
    arrive(2)
    deltas = early(pairs[0])
    for place in range(1, len(pairs)):
        before_it = pairs[place - 1]
        for i in range(before_it, before_it + PAIR):
            give(ob, att_ref, o_s, o_r, i).start()
        if place + split - 1 < len(pairs):
            prepare(place + split - 1)
        late(before_it, deltas)
        deltas = early(pairs[place])
        for i in range(before_it, before_it + PAIR):
            give(gqb, gq_ref, g_s, g_r, i).start()
    final = pairs[-1]
    for i in range(final, final + PAIR):
        give(ob, att_ref, o_s, o_r, i).start()
    late(final, deltas)

    def gradients(n, lo, hi):
        at = slice(lo, hi)
        if n == 0:
            part[0, at, :] = dot(jnp.concatenate([buf[at, :] for buf in dsall], axis=1), qall[...]) * SCALE
        else:
            got = gotf if hi == SHARD else gotn
            part[1, at, :] = dot(jnp.concatenate([buf[at, :] for buf in eall], axis=1), got[...], NT)

    halves = [(n, pl.ds(half * 128, 128), half * 2 + n) for half in range(2) for n in (1, 0)]
    relays = [
        [
            remote(sendk.at[step, n, at], recvk.at[step, n, at], w_s.at[step, place], w_r.at[step, place], (before, h))
            for n, at, place in halves
        ]
        for step in range(REACH)
    ]
    gradients(1, 0, SHARD)
    gradients(0, 0, SHARD)
    for (n, at, place), copy in zip(halves, relays[0]):
        sendk[0, n, at] = part[n, at, :].astype(BF16)

        @pl.when(c > 0)
        def _(copy=copy):
            copy.start()

    for i in range(final, final + PAIR):
        give(gqb, gq_ref, g_s, g_r, i).start()
    gradients(1, SHARD, WIN)
    gradients(0, SHARD, WIN)
    for copy in sends:
        copy.wait_send()

    @pl.when(c < shards - 1)
    def _():
        for step in range(REACH):
            for copy in steps[step]:
                copy.wait_send()

    last = []
    for step in range(REACH):
        for spot, (n, at, place) in enumerate(halves):

            @pl.when(c < shards - 1)
            def _(copy=relays[step][spot]):
                copy.wait_recv()

            mine = pl.ds((step + 1) * SHARD + at.start, 128)
            total = (recvk[step, n, at].astype(F32) + part[n, mine, :]).astype(BF16)
            if step < REACH - 1:
                sendk[step + 1, n, at] = total

                @pl.when(c > 0)
                def _(copy=relays[step + 1][spot]):
                    copy.start()
            else:
                fin[n, at] = total
    outs = (gk_ref, gv_ref)
    for n, out in enumerate(outs):
        copy = pltpu.make_async_copy(fin.at[n, rows_of(h)], out.at[:, narrow(h)], f_r.at[0, n])
        copy.start()
        for i in range(1, PEERS):
            p = to(i)
            copy = remote(fin.at[n, rows_of(p)], out.at[:, narrow(h)], f_s.at[i, n], f_r.at[i, n], (c, p))
            copy.start()
            last.append(copy)

    @pl.when(c > 0)
    def _():
        for step in range(REACH):
            for copy in relays[step]:
                copy.wait_send()

    for i in range(1, PEERS):
        give(ob, att_ref, o_s, o_r, i).wait_send()
        give(gqb, gq_ref, g_s, g_r, i).wait_send()
    for i in range(PEERS):
        for ref, sem in ((att_ref, o_r), (gq_ref, g_r)):
            piece = ref.at[:, wide(to(i))]
            pltpu.make_async_copy(piece, piece, sem.at[i]).wait()
    for copy in last:
        copy.wait_send()
    for i in range(PEERS):
        for n, ref in enumerate(outs):
            piece = ref.at[:, narrow(source(i))]
            pltpu.make_async_copy(piece, piece, f_r.at[i, n]).wait()


def finish(*refs):
    sources, outs, held, sem = refs[:4], refs[4:8], refs[8:12], refs[12]
    into = [pltpu.make_async_copy(sources[n], held[n], sem.at[0, n]) for n in range(4)]
    back = [pltpu.make_async_copy(held[n], outs[n], sem.at[1, n]) for n in range(4)]
    for copy in into:
        copy.start()
    for arrived, copy in zip(into, back):
        arrived.wait()
        copy.start()
    for copy in back:
        copy.wait()


def body(queries, keys, values, documents, grad_out):
    held = pl.BlockSpec(memory_space=pltpu.HBM)
    dma = pltpu.SemaphoreType.DMA
    parts = pl.pallas_call(
        kernel,
        out_shape=(
            jax.ShapeDtypeStruct((ROWS, PEERS * GW), BF16),
            jax.ShapeDtypeStruct((ROWS, PEERS * GW), BF16),
            jax.ShapeDtypeStruct((ROWS, PEERS * HD), BF16),
            jax.ShapeDtypeStruct((ROWS, PEERS * HD), BF16),
        ),
        in_specs=[held, held, held, pl.BlockSpec(memory_space=pltpu.VMEM), held],
        out_specs=(held,) * 4,
        scratch_shapes=[
            pltpu.VMEM((PEERS, ROWS, GW), BF16),
            pltpu.VMEM((PEERS, ROWS, GW), BF16),
            pltpu.VMEM((WIN, HD), BF16),
            pltpu.VMEM((WIN, HD), BF16),
            pltpu.VMEM((HD, WIN), BF16),
            pltpu.VMEM((HD, WIN), BF16),
            pltpu.VMEM((2048, HD), BF16),
            pltpu.VMEM((HD, 2048), BF16),
            pltpu.VMEM((HD, 2048), BF16),
            pltpu.VMEM((WIN, 128), F32),
            pltpu.VMEM((PEERS, WIN, 128), F32),
            pltpu.VMEM((PEERS, ROWS, GW), BF16),
            pltpu.VMEM((PEERS, ROWS, GW), BF16),
            pltpu.VMEM((PEERS, HD, 256), F32),
            pltpu.VMEM((PEERS, HD, 256), F32),
            pltpu.VMEM((PEERS, 8, 256), F32),
            pltpu.VMEM((2, WIN, HD), F32),
            pltpu.VMEM((REACH, 2, SHARD, HD), BF16),
            pltpu.VMEM((REACH, 2, SHARD, HD), BF16),
            pltpu.VMEM((2, SHARD, HD), BF16),
            dma((PEERS, 2)), dma((PEERS, 2)),
            dma((PEERS, 2)), dma((PEERS, 2)),
            dma((REACH, 2 * PEERS)), dma((REACH, 2 * PEERS)),
            dma((PEERS,)), dma((PEERS,)),
            dma((PEERS,)), dma((PEERS,)),
            dma((REACH, 4)), dma((REACH, 4)),
            dma((PEERS, 2)), dma((PEERS, 2)),
            *[pltpu.VMEM((WIN, 256), F32)] * (2 * PAIR),
            *[pltpu.VMEM((WIN, 256), BF16)] * (2 * PEERS),
        ],
        compiler_params=pltpu.CompilerParams(
            collective_id=0, has_side_effects=True, vmem_limit_bytes=67043328
        ),
    )(queries, keys, values, documents.reshape(128, 128), grad_out)
    return pl.pallas_call(
        finish,
        out_shape=[jax.ShapeDtypeStruct(part.shape, BF16) for part in parts],
        in_specs=[held] * 4,
        out_specs=[held] * 4,
        scratch_shapes=[pltpu.VMEM(part.shape, BF16) for part in parts] + [dma((2, 4))],
    )(*parts)


def solution(mesh):
    split = P(("ctx", "kvh"), None)
    return jax.shard_map(
        body,
        mesh=mesh,
        in_specs=(split, split, split, P(), split),
        out_specs=(split,) * 4,
        check_vma=False,
    )
```
